1024 devices in a mesh: energy: 128 (over z_hi, y, x, core), mom: 8 (over z_lo).
Axes of the slice: x: 4, y: 4, z: 32 (z_hi: 4, z_lo: 8; z = z_hi * 8 + z_lo), core: 2. Of those that a mesh axis runs over, the one named last changes fastest.
Arguments:
- green: bfloat16 [8, 128, 4, 2, 128, 128], P('mom', 'energy'), may hold values from -6 to 6
- grad: bfloat16 [8, 4, 2, 2, 128, 128], P('mom'), may hold values from -0.375 to 0.375
- coupling: float32 [8, 4], replicated, may hold values from 0.05 to 0.3
- occupation: float32 [4], replicated, may hold values from 0.1 to 2
- offsets: int32 [4], replicated, may hold values from 1 to 4, as said below
- neighbours: int32 [4, 2], replicated, may hold values from 0 to 3
- qtable: int32 [8, 8], P('mom'), may hold values from 0 to 7
Outputs:
- sigma: float32 [8, 128, 4, 2, 128, 128], P('mom', 'energy')
The draws below stay inside these ranges and needn't reach their ends.
Inputs may be any that keep to these rules, and one draw needn't show every extreme that they name: `offsets`: some mode has offset 1 and some mode has offset 4.
All inputs are finite; a program needn't handle non-finite values.
Results may differ from the reference program's by a relative error of at most 0.0029.
Values may be sent and summed in bfloat16 or wider, within the bound.
No kernel may reach another device: no remote copies, remote signals or barrier semaphores. Data moves between devices by JAX's collectives and lax.ppermute only.
A program may use at most 32 MiB of HBM per device.

```python
import math
import jax
import jax.numpy as jnp
from jax import lax

ORB = 128
CLUST = 4
MODES = 4
NBR = 2
MAXOFF = 4
K = 8
NE = 128


def draw_offsets(key, part):
    key = jax.random.fold_in(key, 11)
    first_key, second_key = jax.random.split(key)
    others = jax.random.randint(first_key, (MODES - 2,), 1, MAXOFF + 1).astype(jnp.int32)
    ends = jnp.array([1, MAXOFF], jnp.int32)
    values = jnp.concatenate([ends, others])
    order = jax.random.permutation(second_key, MODES)
    return values[order].astype(jnp.int32)


def draw_qtable(key, part):
    key = jax.random.fold_in(key, 23)
    return jax.random.randint(key, (K, K), 0, K).astype(jnp.int32)


def set_ends(values, key, low, top_value):
    dims = values.shape
    spot = [jax.random.randint(jax.random.fold_in(key, axis), (), 0, dims[axis]) for axis in range(len(dims))]
    values = values.at[tuple(spot)].set(low)
    longest = dims.index(max(dims))
    spot[longest] = (spot[longest] + 1) % dims[longest]
    return values.at[tuple(spot)].set(top_value)


def block_levels(own_key, dims, shards, least, high):
    def one(axis_at, shards_of):
        steps = jax.random.uniform(jax.random.fold_in(jax.random.fold_in(own_key, 6), axis_at), (shards_of,), jnp.float32, least / len(shards), high / len(shards))
        return jnp.repeat(jnp.exp(steps), dims[axis_at] // shards_of).reshape((-1,) + (1,) * (len(dims) - axis_at - 1))

    gain = one(*shards[0])
    for cut in shards[1:]:
        gain = gain * one(*cut)
    return gain


def centred(own_key, extent, spread, bound, pieces=(), kind=jnp.bfloat16):
    drawn = jax.random.normal(own_key, extent, jnp.float32) * spread
    if len(pieces) > 0:
        drawn = block_levels(own_key, extent, pieces, -0.22, 0.18) * drawn
    return jnp.clip(drawn, min=-bound, max=bound).astype(kind)


def setup_inputs(seed: int = 0) -> dict:
    arg_keys = jax.random.split(jax.random.key(seed), 8)
    return {
        "green": centred(arg_keys[0], (K, NE, CLUST, 2, ORB, ORB), 1.0, 6.0, ((0, 8), (1, 128))),
        "grad": centred(arg_keys[1], (K, CLUST, NBR, 2, ORB, ORB), (2 * ORB) ** -0.5, 0.375, ((0, 8),)),
        "coupling": jnp.clip(jnp.exp(jax.random.uniform(arg_keys[2], (K, MODES), jnp.float32, math.log(0.05), math.log(0.3))), 0.05, 0.3),
        "occupation": jnp.clip(jnp.exp(jax.random.uniform(arg_keys[3], (MODES,), jnp.float32, math.log(0.1), math.log(2.0))), 0.1, 2.0),
        "offsets": draw_offsets(jax.random.fold_in(arg_keys[7], 71), 0),
        "neighbours": set_ends(jax.random.randint(arg_keys[5], (CLUST, NBR), 0, CLUST), jax.random.fold_in(arg_keys[5], 1), 0, CLUST - 1).astype(jnp.int32),
        "qtable": draw_qtable(jax.random.fold_in(arg_keys[7], 71), 0),
    }


def energy_terms(blocks, grad, pick, weights):
    high = lax.Precision.HIGHEST
    chosen = jnp.einsum('csx,jxrab->jcsrab', pick, blocks.astype(jnp.float32), precision=high).astype(jnp.bfloat16).astype(jnp.float32)
    grad_re = grad[:, :, :, 0].astype(jnp.float32)
    grad_im = grad[:, :, :, 1].astype(jnp.float32)
    chosen_re = chosen[:, :, :, 0]
    chosen_im = chosen[:, :, :, 1]
    prod_re = jnp.einsum('kcsab,jcsbd->kjcsad', grad_re, chosen_re, precision=high) - jnp.einsum('kcsab,jcsbd->kjcsad', grad_im, chosen_im, precision=high)
    prod_im = jnp.einsum('kcsab,jcsbd->kjcsad', grad_re, chosen_im, precision=high) + jnp.einsum('kcsab,jcsbd->kjcsad', grad_im, chosen_re, precision=high)
    prod_re = prod_re.astype(jnp.bfloat16).astype(jnp.float32)
    prod_im = prod_im.astype(jnp.bfloat16).astype(jnp.float32)
    triple_re = jnp.einsum('kjcsad,kcsed->kjcsae', prod_re, grad_re, precision=high) + jnp.einsum('kjcsad,kcsed->kjcsae', prod_im, grad_im, precision=high)
    triple_im = jnp.einsum('kjcsad,kcsed->kjcsae', prod_im, grad_re, precision=high) - jnp.einsum('kjcsad,kcsed->kjcsae', prod_re, grad_im, precision=high)
    accum_re = jnp.einsum('kjn,kjcsae->kncae', weights, triple_re, precision=high)
    accum_im = jnp.einsum('kjn,kjcsae->kncae', weights, triple_im, precision=high)
    return jnp.stack([accum_re, accum_im], axis=3)


def reference(green, grad, coupling, occupation, offsets, neighbours, qtable):
    pick = (neighbours[:, :, None] == jnp.arange(CLUST, dtype=jnp.int32)[None, None, :]).astype(jnp.float32)
    weights = coupling[qtable]
    padded = jnp.zeros((K, NE + 2 * MAXOFF, CLUST, 2, ORB, ORB), jnp.float32)

    def step(energy, padded):
        blocks = lax.dynamic_index_in_dim(green, energy, 1, keepdims=False)
        accum = energy_terms(blocks, grad, pick, weights)
        for mode in range(MODES):
            term = accum[:, mode][:, None]
            upper = (energy + MAXOFF + offsets[mode]).astype(jnp.int32)
            lower = (energy + MAXOFF - offsets[mode]).astype(jnp.int32)
            zero = jnp.zeros((), jnp.int32)
            old = lax.dynamic_slice(padded, (zero, upper, zero, zero, zero, zero), term.shape)
            padded = lax.dynamic_update_slice(padded, old + (1.0 + occupation[mode]) * term, (zero, upper, zero, zero, zero, zero))
            old = lax.dynamic_slice(padded, (zero, lower, zero, zero, zero, zero), term.shape)
            padded = lax.dynamic_update_slice(padded, old + occupation[mode] * term, (zero, lower, zero, zero, zero, zero))
        return padded

    padded = lax.fori_loop(0, NE, step, padded)
    return padded[:, MAXOFF:MAXOFF + NE]
```

```python
import jax
import jax.numpy as jnp
from jax import lax
from jax.experimental import pallas as pl
from jax.experimental.pallas import tpu as pltpu
from jax.sharding import Mesh
from jax.sharding import PartitionSpec as P

PLANE = ("y", "x", "core")
LINE = ("zh", "mom")


def mix_kernel(coupling, occupation, offsets, qtable, before, here, after, out, window, terms):
    momenta, quad = here.shape[:2]
    modes = occupation.shape[0]
    for j in range(momenta):
        for i in range(quad):
            window[j, i] = before[j, i].astype(jnp.float32)
            window[j, quad + i] = here[j, i].astype(jnp.float32)
            window[j, 2 * quad + i] = after[j, i].astype(jnp.float32)
    for m in range(modes):
        absorb = occupation[m]
        emit = 1.0 + absorb
        shift = offsets[m]
        for j in range(momenta):
            for i in range(quad):
                terms[m, j, i] = emit * window[j, quad + i - shift] + absorb * window[j, quad + i + shift]

    def one(k, carry):
        total = [jnp.zeros(here.shape[2:], jnp.float32) for _ in range(quad)]
        for j in range(momenta):
            row = qtable[k, j]
            for m in range(modes):
                weight = coupling[row, m]
                for i in range(quad):
                    total[i] = total[i] + weight * terms[m, j, i]
        for i in range(quad):
            out[k, i] = total[i].astype(out.dtype)
        return carry

    lax.fori_loop(0, momenta, one, 0)


def mixed(coupling, occupation, offsets, qtable, before, here, after):
    smem = pl.BlockSpec(memory_space=pltpu.SMEM)
    vmem = pl.BlockSpec(memory_space=pltpu.VMEM)
    momenta, quad, rows, lanes = here.shape
    modes = occupation.shape[0]
    return pl.pallas_call(
        mix_kernel,
        out_shape=jax.ShapeDtypeStruct(here.shape, jnp.bfloat16),
        in_specs=[smem] * 4 + [vmem] * 3,
        out_specs=vmem,
        scratch_shapes=[
            pltpu.VMEM((momenta, 3 * quad, rows, lanes), jnp.float32),
            pltpu.VMEM((modes, momenta, quad, rows, lanes), jnp.float32),
        ],
    )(coupling, occupation, offsets, qtable, before, here, after)


def dress_kernel(neighbours, grad, mixed_ref, out):
    clusters, listed = grad.shape[:2]
    for c in range(clusters):
        total = None
        for s in range(listed):
            near = neighbours[c, s]
            re = mixed_ref[near, 0]
            im = mixed_ref[near, 1]
            d_re = grad[c, s, 0]
            d_im = grad[c, s, 1]
            left = jnp.concatenate([d_re, d_im], axis=1)
            middle = jnp.concatenate(
                [jnp.concatenate([re, im], axis=1), jnp.concatenate([-im, re], axis=1)], axis=0
            )
            right = jnp.concatenate([left, jnp.concatenate([-d_im, d_re], axis=1)], axis=0)
            prod = jnp.dot(left, middle, preferred_element_type=jnp.float32)
            high = prod.astype(jnp.bfloat16)
            low = (prod - high.astype(jnp.float32)).astype(jnp.bfloat16)
            part = lax.dot_general(
                high, right, (((1,), (1,)), ((), ())), preferred_element_type=jnp.float32
            ) + lax.dot_general(
                low, right, (((1,), (1,)), ((), ())), preferred_element_type=jnp.float32
            )
            total = part if total is None else total + part
        orbits = out.shape[-1]
        out[c, 0] = total[:, :orbits]
        out[c, 1] = total[:, orbits:]


def dressed(neighbours, grad, mixed_blocks):
    smem = pl.BlockSpec(memory_space=pltpu.SMEM)
    vmem = pl.BlockSpec(memory_space=pltpu.VMEM)
    return pl.pallas_call(
        dress_kernel,
        out_shape=jax.ShapeDtypeStruct(mixed_blocks.shape, jnp.float32),
        in_specs=[smem, vmem, vmem],
        out_specs=vmem,
    )(neighbours, grad, mixed_blocks)


def swap(x, axis):
    return lax.all_to_all(x, axis, split_axis=0, concat_axis=0, tiled=True)


def shards(green, grad, coupling, occupation, offsets, neighbours, qtable):
    clusters, parts, orbits = green.shape[2:5]
    momenta = lax.axis_size("mom")
    plane = lax.axis_size("y") * lax.axis_size("x") * lax.axis_size("core")
    quads = lax.axis_size("zh") * momenta
    rows = clusters * parts * orbits // plane
    quad = plane // momenta
    table = swap(jnp.broadcast_to(qtable, (momenta, momenta)), "mom")
    pieces = swap(green.reshape(plane, rows, orbits), PLANE)
    here = swap(pieces, "mom")
    before = lax.ppermute(here, LINE, [(z, z + 1) for z in range(quads - 1)])
    after = lax.ppermute(here, LINE, [(z + 1, z) for z in range(quads - 1)])
    shape = (momenta, quad, rows, orbits)
    total = mixed(
        coupling, occupation, offsets, table,
        before.reshape(shape), here.reshape(shape), after.reshape(shape),
    )
    total = swap(swap(total.reshape(plane, rows, orbits), "mom"), PLANE)
    out = dressed(neighbours, grad[0], total.reshape(clusters, parts, orbits, orbits))
    return out[None, None]


def solution(mesh):
    split = Mesh(mesh.devices.reshape(4, 4, 4, 2, 8), ("zh", "y", "x", "core", "mom"))
    energy = ("zh", "y", "x", "core")
    in_specs = (
        P("mom", energy, None, None, None, None),
        P("mom", None, None, None, None, None),
        P(),
        P(),
        P(),
        P(),
        P("mom", None),
    )
    out_specs = P("mom", energy, None, None, None, None)
    return jax.shard_map(shards, mesh=split, in_specs=in_specs, out_specs=out_specs, check_vma=False)
```

```python
import jax
import jax.numpy as jnp
from jax import lax
from jax.experimental import pallas as pl
from jax.experimental.pallas import tpu as pltpu
from jax.sharding import Mesh
from jax.sharding import PartitionSpec as P


PLANE = ("y", "x", "core")
LINE = ("zh", "mom")


def mix_kernel(coupling, occupation, offsets, table, before, here, after, out, window, terms, mixed, sems, done):
    momenta, quad = here.shape[:2]
    modes = occupation.shape[0]
    me = lax.axis_index("mom")
    copies = [
        pltpu.make_async_copy(source, window.at[:, pl.ds(n * quad, quad)], sems.at[n])
        for n, source in enumerate((before, here, after))
    ]
    for copy in copies:
        copy.start()
    for copy in copies:
        copy.wait()
    for m in range(modes):
        absorb = occupation[m]
        emit = 1.0 + absorb
        shift = offsets[m]
        for j in range(momenta):
            for i in range(quad):
                lower = window[j, quad + i - shift].astype(jnp.float32)
                upper = window[j, quad + i + shift].astype(jnp.float32)
                terms[m, j, i] = emit * lower + absorb * upper

    def one(k, carry):
        total = [jnp.zeros(here.shape[2:], jnp.float32) for _ in range(quad)]
        for j in range(momenta):
            row = table[k ^ me, j]
            for m in range(modes):
                weight = coupling[row, m]
                for i in range(quad):
                    total[i] = total[i] + weight * terms[m, j, i]
        for i in range(quad):
            mixed[k, i] = total[i].astype(mixed.dtype)
        return carry

    lax.fori_loop(0, momenta, one, 0)
    copy = pltpu.make_async_copy(mixed, out, done)
    copy.start()
    copy.wait()


def mixed(coupling, occupation, offsets, table, before, here, after):
    smem = pl.BlockSpec(memory_space=pltpu.SMEM)
    free = pl.BlockSpec(memory_space=pl.ANY)
    momenta, quad, rows, lanes = here.shape
    modes = occupation.shape[0]
    return pl.pallas_call(
        mix_kernel,
        out_shape=jax.ShapeDtypeStruct(here.shape, jnp.bfloat16),
        in_specs=[smem] * 4 + [free] * 3,
        out_specs=free,
        scratch_shapes=[
            pltpu.VMEM((momenta, 3 * quad, rows, lanes), jnp.bfloat16),
            pltpu.VMEM((modes, momenta, quad, rows, lanes), jnp.float32),
            pltpu.VMEM((momenta, quad, rows, lanes), jnp.bfloat16),
            pltpu.SemaphoreType.DMA((3,)),
            pltpu.SemaphoreType.DMA,
        ],
        compiler_params=pltpu.CompilerParams(vmem_limit_bytes=16 << 20),
    )(coupling, occupation, offsets, table, before, here, after)


def dress_kernel(neighbours, grad, mixed_in, out, near, slopes, result, sems, done):
    clusters, listed = grad.shape[:2]
    orbits = out.shape[-1]
    first = pltpu.make_async_copy(mixed_in, near, sems.at[clusters])
    copies = [pltpu.make_async_copy(grad.at[c], slopes.at[c], sems.at[c]) for c in range(clusters)]
    first.start()
    for copy in copies:
        copy.start()
    first.wait()
    results = []
    for c in range(clusters):
        copies[c].wait()
        total = None
        for s in range(listed):
            spot = neighbours[c, s]
            re = near[spot, 0]
            im = near[spot, 1]
            d_re = slopes[c, s, 0]
            d_im = slopes[c, s, 1]
            left = jnp.concatenate([d_re, d_im], axis=1)
            middle = jnp.concatenate(
                [jnp.concatenate([re, im], axis=1), jnp.concatenate([-im, re], axis=1)], axis=0
            )
            right = jnp.concatenate([left, jnp.concatenate([-d_im, d_re], axis=1)], axis=0)
            prod = jnp.dot(left, middle, preferred_element_type=jnp.float32)
            high = prod.astype(jnp.bfloat16)
            low = (prod - high.astype(jnp.float32)).astype(jnp.bfloat16)
            part = lax.dot_general(
                jnp.concatenate([high, low], axis=0),
                right,
                (((1,), (1,)), ((), ())),
                preferred_element_type=jnp.float32,
            )
            part = part[:orbits] + part[orbits:]
            total = part if total is None else total + part
        result[c, 0] = total[:, :orbits]
        result[c, 1] = total[:, orbits:]
        copy = pltpu.make_async_copy(result.at[c], out.at[c], done.at[c])
        copy.start()
        results.append(copy)
    for copy in results:
        copy.wait()


def dressed(neighbours, grad, mixed_blocks):
    smem = pl.BlockSpec(memory_space=pltpu.SMEM)
    free = pl.BlockSpec(memory_space=pl.ANY)
    clusters = grad.shape[0]
    return pl.pallas_call(
        dress_kernel,
        out_shape=jax.ShapeDtypeStruct(mixed_blocks.shape, jnp.float32),
        in_specs=[smem, free, free],
        out_specs=free,
        scratch_shapes=[
            pltpu.VMEM(mixed_blocks.shape, mixed_blocks.dtype),
            pltpu.VMEM(grad.shape, grad.dtype),
            pltpu.VMEM(mixed_blocks.shape, jnp.float32),
            pltpu.SemaphoreType.DMA((clusters + 1,)),
            pltpu.SemaphoreType.DMA((clusters,)),
        ],
        compiler_params=pltpu.CompilerParams(vmem_limit_bytes=16 << 20),
    )(neighbours, grad, mixed_blocks)


def swap(x, axis):
    return lax.all_to_all(x, axis, split_axis=0, concat_axis=0, tiled=True)


def paired(x, bit, momenta):
    other = lax.ppermute(x, "mom", [(k, k ^ bit) for k in range(momenta)])
    return jnp.concatenate([x, other])


def shards(green, grad, coupling, occupation, offsets, neighbours, qtable):
    clusters, parts, orbits = green.shape[2:5]
    momenta = lax.axis_size("mom")
    plane = lax.axis_size("y") * lax.axis_size("x") * lax.axis_size("core")
    quads = lax.axis_size("zh") * momenta
    rows = clusters * parts * orbits // plane
    quad = plane // momenta
    pieces = swap(green.reshape(plane, rows, orbits), PLANE)
    table = paired(qtable, 1, momenta)
    table = paired(table, 2, momenta)
    here = swap(pieces, "mom")
    table = paired(table, 4, momenta)
    before = lax.ppermute(here, LINE, [(z, z + 1) for z in range(quads - 1)])
    after = lax.ppermute(here, LINE, [(z + 1, z) for z in range(quads - 1)])
    shape = (momenta, quad, rows, orbits)
    total = mixed(
        coupling, occupation, offsets, table,
        before.reshape(shape), here.reshape(shape), after.reshape(shape),
    )
    total = swap(swap(total.reshape(plane, rows, orbits), "mom"), PLANE)
    out = dressed(neighbours, grad[0], total.reshape(clusters, parts, orbits, orbits))
    return out[None, None]


def solution(mesh):
    split = Mesh(mesh.devices.reshape(4, 4, 4, 2, 8), ("zh", "y", "x", "core", "mom"))
    energy = ("zh", "y", "x", "core")
    in_specs = (
        P("mom", energy, None, None, None, None),
        P("mom", None, None, None, None, None),
        P(),
        P(),
        P(),
        P(),
        P("mom", None),
    )
    out_specs = P("mom", energy, None, None, None, None)
    return jax.shard_map(shards, mesh=split, in_specs=in_specs, out_specs=out_specs, check_vma=False)
```

```python
import jax
import jax.numpy as jnp
from jax import lax
from jax.experimental import pallas as pl
from jax.experimental.pallas import tpu as pltpu
from jax.sharding import Mesh
from jax.sharding import PartitionSpec as P


PLANE = ("y", "x", "core")
LINE = ("zh", "mom")


def mix_kernel(coupling, rates, table, before, here, after, out, terms):
    momenta, quad = here.shape[:2]
    modes = rates.shape[1]
    me = lax.axis_index("mom")

    def term(m, carry):
        emit = rates[0, m]
        absorb = rates[1, m]
        for level in range(1, quad + 1):

            @pl.when(table[momenta, m] == level)
            def _():
                for j in range(momenta):
                    for i in range(quad):
                        down = here[j, i - level] if i >= level else before[j, quad + i - level]
                        up = here[j, i + level] if i + level < quad else after[j, i + level - quad]
                        terms[m, j, i] = emit * down.astype(jnp.float32) + absorb * up.astype(jnp.float32)

        return carry

    lax.fori_loop(0, modes, term, 0)

    def one(k, carry):
        total = [jnp.zeros(here.shape[2:], jnp.float32) for _ in range(quad)]
        far = k ^ me
        spot = (far >> 2) + (far & 2) + ((far & 1) << 2)
        for j in range(momenta):
            row = table[spot, j]
            for m in range(modes):
                weight = coupling[row, m]
                for i in range(quad):
                    total[i] = total[i] + weight * terms[m, j, i]
        for i in range(quad):
            out[k, i] = total[i].astype(out.dtype)
        return carry

    lax.fori_loop(0, momenta, one, 0)


def mixed(coupling, rates, table, before, here, after):
    smem = pl.BlockSpec(memory_space=pltpu.SMEM)
    vmem = pl.BlockSpec(memory_space=pltpu.VMEM)
    momenta, quad, rows, lanes = here.shape
    modes = rates.shape[1]
    return pl.pallas_call(
        mix_kernel,
        out_shape=jax.ShapeDtypeStruct(here.shape, jnp.bfloat16),
        in_specs=[smem] * 3 + [vmem] * 3,
        out_specs=vmem,
        scratch_shapes=[pltpu.VMEM((modes, momenta, quad, rows, lanes), jnp.float32)],
        compiler_params=pltpu.CompilerParams(vmem_limit_bytes=16 << 20),
    )(coupling, rates, table, before, here, after)


def dress_kernel(neighbours, grad, near, out, result, done):
    clusters, listed = grad.shape[:2]
    orbits = out.shape[-1]
    copies = []
    for c in range(clusters):
        total = None
        for s in range(listed):
            spot = neighbours[c, s]
            re = near[spot, 0]
            im = near[spot, 1]
            d_re = grad[c, s, 0]
            d_im = grad[c, s, 1]
            left = jnp.concatenate([d_re, d_im], axis=1)
            middle = jnp.concatenate(
                [jnp.concatenate([re, im], axis=1), jnp.concatenate([-im, re], axis=1)], axis=0
            )
            right = jnp.concatenate([left, jnp.concatenate([-d_im, d_re], axis=1)], axis=0)
            prod = jnp.dot(left, middle, preferred_element_type=jnp.float32)
            high = prod.astype(jnp.bfloat16)
            low = (prod - high.astype(jnp.float32)).astype(jnp.bfloat16)
            part = lax.dot_general(
                jnp.concatenate([high, low], axis=0),
                right,
                (((1,), (1,)), ((), ())),
                preferred_element_type=jnp.float32,
            )
            part = part[:orbits] + part[orbits:]
            total = part if total is None else total + part
        result[c, 0] = total[:, :orbits]
        result[c, 1] = total[:, orbits:]
        copy = pltpu.make_async_copy(result.at[c], out.at[c], done.at[c])
        copy.start()
        copies.append(copy)
    for copy in copies:
        copy.wait()


def dressed(neighbours, grad, mixed_blocks):
    smem = pl.BlockSpec(memory_space=pltpu.SMEM)
    vmem = pl.BlockSpec(memory_space=pltpu.VMEM)
    clusters = grad.shape[0]
    return pl.pallas_call(
        dress_kernel,
        out_shape=jax.ShapeDtypeStruct(mixed_blocks.shape, jnp.float32),
        in_specs=[smem, vmem, vmem],
        out_specs=pl.BlockSpec(memory_space=pl.ANY),
        scratch_shapes=[
            pltpu.VMEM(mixed_blocks.shape, jnp.float32),
            pltpu.SemaphoreType.DMA((clusters,)),
        ],
        compiler_params=pltpu.CompilerParams(vmem_limit_bytes=16 << 20),
    )(neighbours, grad, mixed_blocks)


def swap(x, axis):
    return lax.all_to_all(x, axis, split_axis=0, concat_axis=0, tiled=True)


def paired(x, bit, momenta):
    other = lax.ppermute(x, "mom", [(k, k ^ bit) for k in range(momenta)])
    return jnp.concatenate([x, other])


def shards(green, grad, coupling, occupation, offsets, neighbours, qtable):
    clusters, parts, orbits = green.shape[2:5]
    momenta = lax.axis_size("mom")
    plane = lax.axis_size("y") * lax.axis_size("x") * lax.axis_size("core")
    quads = lax.axis_size("zh") * momenta
    rows = clusters * parts * orbits // plane
    quad = plane // momenta
    pieces = swap(green.reshape(plane, rows, orbits), PLANE)
    table = paired(qtable, 4, momenta)
    rates = jnp.stack([1.0 + occupation, occupation])
    here = swap(pieces, "mom")
    table = paired(table, 2, momenta)
    before = lax.ppermute(here, LINE, [(z, z + 1) for z in range(quads - 1)])
    after = lax.ppermute(here, LINE, [(z + 1, z) for z in range(quads - 1)])
    table = paired(table, 1, momenta)
    spread = jnp.pad(offsets, (0, momenta - offsets.shape[0]))
    table = jnp.concatenate([table, spread[None]])
    shape = (momenta, quad, rows, orbits)
    total = mixed(
        coupling, rates, table,
        before.reshape(shape), here.reshape(shape), after.reshape(shape),
    )
    total = swap(swap(total.reshape(plane, rows, orbits), "mom"), PLANE)
    out = dressed(neighbours, grad[0], total.reshape(clusters, parts, orbits, orbits))
    return out[None, None]


def solution(mesh):
    split = Mesh(mesh.devices.reshape(4, 4, 4, 2, 8), ("zh", "y", "x", "core", "mom"))
    energy = ("zh", "y", "x", "core")
    in_specs = (
        P("mom", energy, None, None, None, None),
        P("mom", None, None, None, None, None),
        P(),
        P(),
        P(),
        P(),
        P("mom", None),
    )
    out_specs = P("mom", energy, None, None, None, None)
    return jax.shard_map(shards, mesh=split, in_specs=in_specs, out_specs=out_specs, check_vma=False)
```

```python
import jax
import jax.numpy as jnp
from jax import lax
from jax.experimental import pallas as pl
from jax.experimental.pallas import tpu as pltpu
from jax.sharding import Mesh
from jax.sharding import PartitionSpec as P


PLANE = ("y", "x", "core")
LINE = ("zh", "mom")


def mix_kernel(levels, table, before, here, after, out, rows_of):
    momenta, quad, rows, lanes = here.shape
    shifts = levels.shape[0]
    half = rows // 2
    height = momenta * half
    me = lax.axis_index("mom")
    sublane = lax.broadcasted_iota(jnp.int32, (half, lanes), 0)
    lane = lax.broadcasted_iota(jnp.int32, (half, lanes), 1)
    diagonal = sublane == lax.rem(lane, half)
    values = levels[...]
    strengths = [jnp.broadcast_to(values[:, q : q + 1], (shifts, lanes)) for q in range(momenta)]
    for i in range(momenta):
        index = jnp.broadcast_to(table[i : i + 1], (shifts, lanes))
        weight = jnp.zeros((shifts, lanes), jnp.float32)
        for q, strength in enumerate(strengths):
            weight = jnp.where(index == q, strength, weight)
        high = weight.astype(jnp.bfloat16).astype(jnp.float32)
        for n, part in enumerate((high, weight - high)):
            for d in range(shifts):
                spread = jnp.broadcast_to(part[d : d + 1], (half, lanes))
                block = jnp.where(diagonal, spread, 0.0).astype(jnp.bfloat16)
                start = n * height + i * half
                rows_of[start : start + half, d * lanes : (d + 1) * lanes] = block

    def near(j, e):
        if e < 0:
            block = before[j, e + quad]
        elif e < quad:
            block = here[j, e]
        else:
            block = after[j, e - quad]
        return jnp.concatenate([block[:half], block[half:]], axis=1)

    spots = []
    for i in range(momenta):
        spots.append(((i & 1) << 1 | (i & 2) << 1 | (i & 4) >> 2) ^ me)
    for e in range(quad):
        blocks = [near(j, e - level) for level in range(1, quad + 1) for j in range(momenta)]
        blocks += [near(j, e + level) for level in range(1, quad + 1) for j in range(momenta)]
        both = jnp.dot(rows_of[...], jnp.concatenate(blocks, axis=0), preferred_element_type=jnp.float32)
        total = (both[:height] + both[height:]).astype(out.dtype)
        for i in range(momenta):
            piece = total[i * half : (i + 1) * half]
            out[spots[i], e, :half] = piece[:, :lanes]
            out[spots[i], e, half:] = piece[:, lanes:]


def mixed(levels, table, before, here, after):
    vmem = pl.BlockSpec(memory_space=pltpu.VMEM)
    momenta, _, rows, lanes = here.shape
    shifts = levels.shape[0]
    return pl.pallas_call(
        mix_kernel,
        out_shape=jax.ShapeDtypeStruct(here.shape, jnp.bfloat16),
        in_specs=[vmem] * 5,
        out_specs=vmem,
        scratch_shapes=[pltpu.VMEM((momenta * rows, shifts * lanes), jnp.bfloat16)],
        compiler_params=pltpu.CompilerParams(vmem_limit_bytes=16 << 20),
    )(levels, table, before, here, after)


def dress_kernel(neighbours, grad, near, out, result, done):
    clusters, listed = grad.shape[:2]
    orbits = out.shape[-1]
    copies = []
    for c in range(clusters):
        total = None
        for s in range(listed):
            spot = neighbours[c, s]
            re = near[spot, 0]
            im = near[spot, 1]
            d_re = grad[c, s, 0]
            d_im = grad[c, s, 1]
            left = jnp.concatenate([d_re, d_im], axis=1)
            middle = jnp.concatenate(
                [jnp.concatenate([re, im], axis=1), jnp.concatenate([-im, re], axis=1)], axis=0
            )
            right = jnp.concatenate([left, jnp.concatenate([-d_im, d_re], axis=1)], axis=0)
            prod = jnp.dot(left, middle, preferred_element_type=jnp.float32)
            high = prod.astype(jnp.bfloat16)
            low = (prod - high.astype(jnp.float32)).astype(jnp.bfloat16)
            part = lax.dot_general(
                jnp.concatenate([high, low], axis=0),
                right,
                (((1,), (1,)), ((), ())),
                preferred_element_type=jnp.float32,
            )
            part = part[:orbits] + part[orbits:]
            total = part if total is None else total + part
        result[c, 0] = total[:, :orbits]
        result[c, 1] = total[:, orbits:]
        copy = pltpu.make_async_copy(result.at[c], out.at[c], done.at[c])
        copy.start()
        copies.append(copy)
    for copy in copies:
        copy.wait()


def dressed(neighbours, grad, mixed_blocks):
    smem = pl.BlockSpec(memory_space=pltpu.SMEM)
    vmem = pl.BlockSpec(memory_space=pltpu.VMEM)
    clusters = grad.shape[0]
    return pl.pallas_call(
        dress_kernel,
        out_shape=jax.ShapeDtypeStruct(mixed_blocks.shape, jnp.float32),
        in_specs=[smem, vmem, vmem],
        out_specs=pl.BlockSpec(memory_space=pl.ANY),
        scratch_shapes=[
            pltpu.VMEM(mixed_blocks.shape, jnp.float32),
            pltpu.SemaphoreType.DMA((clusters,)),
        ],
        compiler_params=pltpu.CompilerParams(vmem_limit_bytes=16 << 20),
    )(neighbours, grad, mixed_blocks)


def swap(x, axis):
    return lax.all_to_all(x, axis, split_axis=0, concat_axis=0, tiled=True)


def paired(x, bit, momenta):
    other = lax.ppermute(x, "mom", [(k, k ^ bit) for k in range(momenta)])
    return jnp.concatenate([x, other])


def shards(green, grad, coupling, occupation, offsets, neighbours, qtable):
    clusters, parts, orbits = green.shape[2:5]
    momenta = lax.axis_size("mom")
    plane = lax.axis_size("y") * lax.axis_size("x") * lax.axis_size("core")
    quads = lax.axis_size("zh") * momenta
    rows = clusters * parts * orbits // plane
    quad = plane // momenta
    shape = (momenta, quad, rows, orbits)
    pieces = swap(green.reshape(plane, rows, orbits), PLANE)
    rates = jnp.stack([1.0 + occupation, occupation])
    level = jnp.arange(1, quad + 1, dtype=jnp.int32)
    chosen = jnp.where(offsets == level[:, None], rates[:, None], 0.0)
    levels = jnp.sum(chosen[:, :, None] * coupling, axis=-1).reshape(2 * quad, momenta)
    table = paired(jnp.repeat(qtable, orbits // momenta, axis=1), 2, momenta)
    here = swap(pieces, "mom")
    table = paired(table, 4, momenta)
    before = lax.ppermute(here, LINE, [(z, z + 1) for z in range(quads - 1)])
    after = lax.ppermute(here, LINE, [(z + 1, z) for z in range(quads - 1)])
    table = paired(table, 1, momenta)
    total = mixed(levels, table, before.reshape(shape), here.reshape(shape), after.reshape(shape))
    total = swap(swap(total.reshape(plane, rows, orbits), "mom"), PLANE)
    out = dressed(neighbours, grad[0], total.reshape(clusters, parts, orbits, orbits))
    return out[None, None]


def solution(mesh):
    split = Mesh(mesh.devices.reshape(4, 4, 4, 2, 8), ("zh", "y", "x", "core", "mom"))
    energy = ("zh", "y", "x", "core")
    in_specs = (
        P("mom", energy, None, None, None, None),
        P("mom", None, None, None, None, None),
        P(),
        P(),
        P(),
        P(),
        P("mom", None),
    )
    out_specs = P("mom", energy, None, None, None, None)
    return jax.shard_map(shards, mesh=split, in_specs=in_specs, out_specs=out_specs, check_vma=False)
```

```python
import jax
import jax.numpy as jnp
from jax import lax
from jax.experimental import pallas as pl
from jax.experimental.pallas import tpu as pltpu
from jax.sharding import Mesh
from jax.sharding import PartitionSpec as P


PLANE = ("y", "x", "core")
LINE = ("zh", "mom")


def mix_kernel(levels, table, before, here, after, out, rows_of):
    momenta, quad, rows, lanes = here.shape
    shifts = levels.shape[0]
    half = rows // 2
    height = momenta * half
    me = lax.axis_index("mom")
    sublane = lax.broadcasted_iota(jnp.int32, (half, lanes), 0)
    lane = lax.broadcasted_iota(jnp.int32, (half, lanes), 1)
    diagonal = sublane == lax.rem(lane, half)
    values = levels[...]
    strengths = [jnp.broadcast_to(values[:, q : q + 1], (shifts, lanes)) for q in range(momenta)]
    rows_in = table[...]
    owner = lax.broadcasted_iota(jnp.int32, (momenta, lanes), 1) // half
    indices = jnp.zeros((momenta, lanes), jnp.int32)
    for j in range(momenta):
        indices = jnp.where(owner == j, jnp.broadcast_to(rows_in[:, j : j + 1], (momenta, lanes)), indices)
    for i in range(momenta):
        index = jnp.broadcast_to(indices[i : i + 1], (shifts, lanes))
        weight = jnp.zeros((shifts, lanes), jnp.float32)
        for q, strength in enumerate(strengths):
            weight = jnp.where(index == q, strength, weight)
        high = weight.astype(jnp.bfloat16).astype(jnp.float32)
        for n, part in enumerate((high, weight - high)):
            for d in range(shifts):
                spread = jnp.broadcast_to(part[d : d + 1], (half, lanes))
                block = jnp.where(diagonal, spread, 0.0).astype(jnp.bfloat16)
                start = n * height + i * half
                rows_of[start : start + half, d * lanes : (d + 1) * lanes] = block

    def near(j, e):
        if e < 0:
            block = before[j, e + quad]
        elif e < quad:
            block = here[j, e]
        else:
            block = after[j, e - quad]
        return jnp.concatenate([block[:half], block[half:]], axis=1)

    for e in range(quad):
        blocks = [near(j, e - level) for level in range(1, quad + 1) for j in range(momenta)]
        blocks += [near(j, e + level) for level in range(1, quad + 1) for j in range(momenta)]
        both = jnp.dot(rows_of[...], jnp.concatenate(blocks, axis=0), preferred_element_type=jnp.float32)
        total = (both[:height] + both[height:]).astype(out.dtype)
        for i in range(momenta):
            piece = total[i * half : (i + 1) * half]
            out[me ^ i, e, :half] = piece[:, :lanes]
            out[me ^ i, e, half:] = piece[:, lanes:]


def mixed(levels, table, before, here, after):
    vmem = pl.BlockSpec(memory_space=pltpu.VMEM)
    momenta, _, rows, lanes = here.shape
    shifts = levels.shape[0]
    return pl.pallas_call(
        mix_kernel,
        out_shape=jax.ShapeDtypeStruct(here.shape, jnp.bfloat16),
        in_specs=[vmem] * 5,
        out_specs=vmem,
        scratch_shapes=[pltpu.VMEM((momenta * rows, shifts * lanes), jnp.bfloat16)],
        compiler_params=pltpu.CompilerParams(vmem_limit_bytes=16 << 20),
    )(levels, table, before, here, after)


def dress_kernel(neighbours, grad, near, out, result, done):
    clusters, listed = grad.shape[:2]
    orbits = out.shape[-1]
    copies = []
    for c in range(clusters):
        total = None
        for s in range(listed):
            spot = neighbours[c, s]
            re = near[spot, 0]
            im = near[spot, 1]
            d_re = grad[c, s, 0]
            d_im = grad[c, s, 1]
            left = jnp.concatenate([d_re, d_im], axis=1)
            middle = jnp.concatenate(
                [jnp.concatenate([re, im], axis=1), jnp.concatenate([-im, re], axis=1)], axis=0
            )
            right = jnp.concatenate([left, jnp.concatenate([-d_im, d_re], axis=1)], axis=0)
            prod = jnp.dot(left, middle, preferred_element_type=jnp.float32)
            high = prod.astype(jnp.bfloat16)
            low = (prod - high.astype(jnp.float32)).astype(jnp.bfloat16)
            part = lax.dot_general(
                jnp.concatenate([high, low], axis=0),
                right,
                (((1,), (1,)), ((), ())),
                preferred_element_type=jnp.float32,
            )
            part = part[:orbits] + part[orbits:]
            total = part if total is None else total + part
        result[c, 0] = total[:, :orbits]
        result[c, 1] = total[:, orbits:]
        copy = pltpu.make_async_copy(result.at[c], out.at[c], done.at[c])
        copy.start()
        copies.append(copy)
    for copy in copies:
        copy.wait()


def dressed(neighbours, grad, mixed_blocks):
    smem = pl.BlockSpec(memory_space=pltpu.SMEM)
    vmem = pl.BlockSpec(memory_space=pltpu.VMEM)
    clusters = grad.shape[0]
    return pl.pallas_call(
        dress_kernel,
        out_shape=jax.ShapeDtypeStruct(mixed_blocks.shape, jnp.float32),
        in_specs=[smem, vmem, vmem],
        out_specs=pl.BlockSpec(memory_space=pl.ANY),
        scratch_shapes=[
            pltpu.VMEM(mixed_blocks.shape, jnp.float32),
            pltpu.SemaphoreType.DMA((clusters,)),
        ],
        compiler_params=pltpu.CompilerParams(vmem_limit_bytes=16 << 20),
    )(neighbours, grad, mixed_blocks)


def swap(x, axis):
    return lax.all_to_all(x, axis, split_axis=0, concat_axis=0, tiled=True)


def crossed(x, bits, momenta):
    return lax.ppermute(x, "mom", [(k, k ^ bits) for k in range(momenta)])


def shards(green, grad, coupling, occupation, offsets, neighbours, qtable):
    clusters, parts, orbits = green.shape[2:5]
    momenta = lax.axis_size("mom")
    plane = lax.axis_size("y") * lax.axis_size("x") * lax.axis_size("core")
    quads = lax.axis_size("zh") * momenta
    rows = clusters * parts * orbits // plane
    quad = plane // momenta
    shape = (momenta, quad, rows, orbits)
    pieces = swap(green.reshape(plane, rows, orbits), PLANE)
    rates = jnp.stack([1.0 + occupation, occupation])
    level = jnp.arange(1, quad + 1, dtype=jnp.int32)
    chosen = jnp.where(offsets == level[:, None], rates[:, None], 0.0)
    levels = jnp.sum(chosen[:, :, None] * coupling, axis=-1).reshape(2 * quad, momenta)
    rows_in = [qtable]
    for bits in range(1, 4):
        rows_in.append(crossed(qtable, bits, momenta))
    near = jnp.concatenate(rows_in)
    here = swap(pieces, "mom")
    table = jnp.concatenate([near, crossed(near, 4, momenta)])
    before = lax.ppermute(here, LINE, [(z, z + 1) for z in range(quads - 1)])
    after = lax.ppermute(here, LINE, [(z + 1, z) for z in range(quads - 1)])
    total = mixed(levels, table, before.reshape(shape), here.reshape(shape), after.reshape(shape))
    total = swap(swap(total.reshape(plane, rows, orbits), "mom"), PLANE)
    out = dressed(neighbours, grad[0], total.reshape(clusters, parts, orbits, orbits))
    return out[None, None]


def solution(mesh):
    split = Mesh(mesh.devices.reshape(4, 4, 4, 2, 8), ("zh", "y", "x", "core", "mom"))
    energy = ("zh", "y", "x", "core")
    in_specs = (
        P("mom", energy, None, None, None, None),
        P("mom", None, None, None, None, None),
        P(),
        P(),
        P(),
        P(),
        P("mom", None),
    )
    out_specs = P("mom", energy, None, None, None, None)
    return jax.shard_map(shards, mesh=split, in_specs=in_specs, out_specs=out_specs, check_vma=False)
```

```python
import jax
import jax.numpy as jnp
from jax import lax
from jax.experimental import pallas as pl
from jax.experimental.pallas import tpu as pltpu
from jax.sharding import Mesh
from jax.sharding import PartitionSpec as P


PLANE = ("y", "x", "core")
LINE = ("zh", "mom")


def mix_kernel(levels, before, here, after, out, rows_of):
    momenta, quad, rows, lanes = out.shape
    shifts = levels.shape[0]
    half = rows // 2
    height = momenta * half
    sublane = lax.broadcasted_iota(jnp.int32, (half, lanes), 0)
    lane = lax.broadcasted_iota(jnp.int32, (half, lanes), 1)
    diagonal = sublane == lax.rem(lane, half)
    values = levels[...]
    strengths = [jnp.broadcast_to(values[:, q : q + 1], (shifts, lanes)) for q in range(momenta)]
    for k in range(momenta):
        index = here[k, quad * rows :].astype(jnp.float32)
        weight = jnp.zeros((shifts, lanes), jnp.float32)
        for q, strength in enumerate(strengths):
            weight = jnp.where(index == float(q), strength, weight)
        high = weight.astype(jnp.bfloat16).astype(jnp.float32)
        for n, part in enumerate((high, weight - high)):
            for d in range(shifts):
                spread = jnp.broadcast_to(part[d : d + 1], (half, lanes))
                block = jnp.where(diagonal, spread, 0.0).astype(jnp.bfloat16)
                start = n * height + k * half
                rows_of[start : start + half, d * lanes : (d + 1) * lanes] = block

    def near(j, e):
        if e < 0:
            source, e = before, e + quad
        elif e < quad:
            source = here
        else:
            source, e = after, e - quad
        start = e * rows
        return jnp.concatenate(
            [source[j, start : start + half], source[j, start + half : start + rows]], axis=1
        )

    for e in range(quad):
        blocks = [near(j, e - level) for level in range(1, quad + 1) for j in range(momenta)]
        blocks += [near(j, e + level) for level in range(1, quad + 1) for j in range(momenta)]
        both = jnp.dot(rows_of[...], jnp.concatenate(blocks, axis=0), preferred_element_type=jnp.float32)
        total = (both[:height] + both[height:]).astype(out.dtype)
        for k in range(momenta):
            piece = total[k * half : (k + 1) * half]
            out[k, e, :half] = piece[:, :lanes]
            out[k, e, half:] = piece[:, lanes:]


def mixed(levels, before, here, after, shape):
    vmem = pl.BlockSpec(memory_space=pltpu.VMEM)
    momenta, _, rows, lanes = shape
    shifts = levels.shape[0]
    return pl.pallas_call(
        mix_kernel,
        out_shape=jax.ShapeDtypeStruct(shape, jnp.bfloat16),
        in_specs=[vmem] * 4,
        out_specs=vmem,
        scratch_shapes=[pltpu.VMEM((momenta * rows, shifts * lanes), jnp.bfloat16)],
        compiler_params=pltpu.CompilerParams(vmem_limit_bytes=16 << 20),
    )(levels, before, here, after)


def dress_kernel(neighbours, grad, near, out, result, done):
    clusters, listed = grad.shape[:2]
    orbits = out.shape[-1]
    copies = []
    for c in range(clusters):
        total = None
        for s in range(listed):
            spot = neighbours[c, s]
            re = near[spot, 0]
            im = near[spot, 1]
            d_re = grad[c, s, 0]
            d_im = grad[c, s, 1]
            left = jnp.concatenate([d_re, d_im], axis=1)
            middle = jnp.concatenate(
                [jnp.concatenate([re, im], axis=1), jnp.concatenate([-im, re], axis=1)], axis=0
            )
            right = jnp.concatenate([left, jnp.concatenate([-d_im, d_re], axis=1)], axis=0)
            prod = jnp.dot(left, middle, preferred_element_type=jnp.float32)
            high = prod.astype(jnp.bfloat16)
            low = (prod - high.astype(jnp.float32)).astype(jnp.bfloat16)
            part = lax.dot_general(
                jnp.concatenate([high, low], axis=0),
                right,
                (((1,), (1,)), ((), ())),
                preferred_element_type=jnp.float32,
            )
            part = part[:orbits] + part[orbits:]
            total = part if total is None else total + part
        result[c, 0] = total[:, :orbits]
        result[c, 1] = total[:, orbits:]
        copy = pltpu.make_async_copy(result.at[c], out.at[c], done.at[c])
        copy.start()
        copies.append(copy)
    for copy in copies:
        copy.wait()


def dressed(neighbours, grad, mixed_blocks):
    smem = pl.BlockSpec(memory_space=pltpu.SMEM)
    vmem = pl.BlockSpec(memory_space=pltpu.VMEM)
    clusters = grad.shape[0]
    return pl.pallas_call(
        dress_kernel,
        out_shape=jax.ShapeDtypeStruct(mixed_blocks.shape, jnp.float32),
        in_specs=[smem, vmem, vmem],
        out_specs=pl.BlockSpec(memory_space=pl.ANY),
        scratch_shapes=[
            pltpu.VMEM(mixed_blocks.shape, jnp.float32),
            pltpu.SemaphoreType.DMA((clusters,)),
        ],
        compiler_params=pltpu.CompilerParams(vmem_limit_bytes=16 << 20),
    )(neighbours, grad, mixed_blocks)


def swap(x, axis):
    return lax.all_to_all(x, axis, split_axis=0, concat_axis=0, tiled=True)


def shards(green, grad, coupling, occupation, offsets, neighbours, qtable):
    clusters, parts, orbits = green.shape[2:5]
    momenta = lax.axis_size("mom")
    plane = lax.axis_size("y") * lax.axis_size("x") * lax.axis_size("core")
    quads = lax.axis_size("zh") * momenta
    rows = clusters * parts * orbits // plane
    quad = plane // momenta
    shape = (momenta, quad, rows, orbits)
    pieces = swap(green.reshape(plane, rows, orbits), PLANE)
    rates = jnp.stack([1.0 + occupation, occupation])
    level = jnp.arange(1, quad + 1, dtype=jnp.int32)
    chosen = jnp.where(offsets == level[:, None], rates[:, None], 0.0)
    levels = jnp.sum(chosen[:, :, None] * coupling, axis=-1).reshape(2 * quad, momenta)
    row = jnp.repeat(qtable, orbits // momenta, axis=1).astype(green.dtype)
    row = jnp.broadcast_to(row, (momenta, 2 * quad, orbits))
    slabs = jnp.concatenate([pieces.reshape(momenta, quad * rows, orbits), row], axis=1)
    here = swap(slabs, "mom")
    before = lax.ppermute(here, LINE, [(z, z + 1) for z in range(quads - 1)])
    after = lax.ppermute(here, LINE, [(z + 1, z) for z in range(quads - 1)])
    total = mixed(levels, before, here, after, shape)
    total = swap(swap(total.reshape(plane, rows, orbits), "mom"), PLANE)
    out = dressed(neighbours, grad[0], total.reshape(clusters, parts, orbits, orbits))
    return out[None, None]


def solution(mesh):
    split = Mesh(mesh.devices.reshape(4, 4, 4, 2, 8), ("zh", "y", "x", "core", "mom"))
    energy = ("zh", "y", "x", "core")
    in_specs = (
        P("mom", energy, None, None, None, None),
        P("mom", None, None, None, None, None),
        P(),
        P(),
        P(),
        P(),
        P("mom", None),
    )
    out_specs = P("mom", energy, None, None, None, None)
    return jax.shard_map(shards, mesh=split, in_specs=in_specs, out_specs=out_specs, check_vma=False)
```

```python
import jax
import jax.numpy as jnp
from jax import lax
from jax.experimental import pallas as pl
from jax.experimental.pallas import tpu as pltpu
from jax.sharding import Mesh
from jax.sharding import PartitionSpec as P


PLANE = ("y", "x", "core")
LINE = ("zh", "mom")


def mix_kernel(levels, before, here, after, out, rows_of):
    momenta, quad, rows, lanes = out.shape
    shifts = levels.shape[0]
    half = rows // 2
    height = momenta * half
    body = momenta * quad * rows
    me = lax.axis_index("mom")
    sublane = lax.broadcasted_iota(jnp.int32, (half, lanes), 0)
    lane = lax.broadcasted_iota(jnp.int32, (half, lanes), 1)
    diagonal = sublane == lax.rem(lane, half)
    values = levels[...]
    strengths = [jnp.broadcast_to(values[:, q : q + 1], (shifts, lanes)) for q in range(momenta)]
    own = here[body:].astype(jnp.float32)
    lower = before[body:].astype(jnp.float32)
    upper = after[body:].astype(jnp.float32)
    odd = jnp.zeros(own.shape, jnp.int32) + (me & 1)
    partner = jnp.where(odd == 1, lower, upper)
    for i in range(momenta):
        table = partner if i >= momenta // 2 else own
        spot = i % (momenta // 2)
        index = jnp.broadcast_to(table[spot : spot + 1], (shifts, lanes))
        weight = jnp.zeros((shifts, lanes), jnp.float32)
        for q, strength in enumerate(strengths):
            weight = jnp.where(index == float(q), strength, weight)
        high = weight.astype(jnp.bfloat16).astype(jnp.float32)
        for n, part in enumerate((high, weight - high)):
            for d in range(shifts):
                spread = jnp.broadcast_to(part[d : d + 1], (half, lanes))
                block = jnp.where(diagonal, spread, 0.0).astype(jnp.bfloat16)
                start = n * height + i * half
                rows_of[start : start + half, d * lanes : (d + 1) * lanes] = block

    def near(j, e):
        if e < 0:
            source, e = before, e + quad
        elif e < quad:
            source = here
        else:
            source, e = after, e - quad
        start = (j * quad + e) * rows
        return jnp.concatenate([source[start : start + half], source[start + half : start + rows]], axis=1)

    spots = [((i & 1) << 1 | (i & 2) << 1 | (i & 4) >> 2) ^ me for i in range(momenta)]
    for e in range(quad):
        blocks = [near(j, e - level) for level in range(1, quad + 1) for j in range(momenta)]
        blocks += [near(j, e + level) for level in range(1, quad + 1) for j in range(momenta)]
        both = jnp.dot(rows_of[...], jnp.concatenate(blocks, axis=0), preferred_element_type=jnp.float32)
        total = (both[:height] + both[height:]).astype(out.dtype)
        for i in range(momenta):
            piece = total[i * half : (i + 1) * half]
            out[spots[i], e, :half] = piece[:, :lanes]
            out[spots[i], e, half:] = piece[:, lanes:]


def mixed(levels, before, here, after, shape):
    vmem = pl.BlockSpec(memory_space=pltpu.VMEM)
    momenta, _, rows, lanes = shape
    shifts = levels.shape[0]
    return pl.pallas_call(
        mix_kernel,
        out_shape=jax.ShapeDtypeStruct(shape, jnp.bfloat16),
        in_specs=[vmem] * 4,
        out_specs=vmem,
        scratch_shapes=[pltpu.VMEM((momenta * rows, shifts * lanes), jnp.bfloat16)],
        compiler_params=pltpu.CompilerParams(vmem_limit_bytes=16 << 20),
    )(levels, before, here, after)


def dress_kernel(neighbours, grad, near, out, result, done):
    clusters, listed = grad.shape[:2]
    orbits = out.shape[-1]
    copies = []
    for c in range(clusters):
        total = None
        for s in range(listed):
            spot = neighbours[c, s]
            re = near[spot, 0]
            im = near[spot, 1]
            d_re = grad[c, s, 0]
            d_im = grad[c, s, 1]
            left = jnp.concatenate([d_re, d_im], axis=1)
            middle = jnp.concatenate(
                [jnp.concatenate([re, im], axis=1), jnp.concatenate([-im, re], axis=1)], axis=0
            )
            right = jnp.concatenate([left, jnp.concatenate([-d_im, d_re], axis=1)], axis=0)
            prod = jnp.dot(left, middle, preferred_element_type=jnp.float32)
            high = prod.astype(jnp.bfloat16)
            low = (prod - high.astype(jnp.float32)).astype(jnp.bfloat16)
            part = lax.dot_general(
                jnp.concatenate([high, low], axis=0),
                right,
                (((1,), (1,)), ((), ())),
                preferred_element_type=jnp.float32,
            )
            part = part[:orbits] + part[orbits:]
            total = part if total is None else total + part
        result[c, 0] = total[:, :orbits]
        result[c, 1] = total[:, orbits:]
        copy = pltpu.make_async_copy(result.at[c], out.at[c], done.at[c])
        copy.start()
        copies.append(copy)
    for copy in copies:
        copy.wait()


def dressed(neighbours, grad, mixed_blocks):
    smem = pl.BlockSpec(memory_space=pltpu.SMEM)
    vmem = pl.BlockSpec(memory_space=pltpu.VMEM)
    clusters = grad.shape[0]
    return pl.pallas_call(
        dress_kernel,
        out_shape=jax.ShapeDtypeStruct(mixed_blocks.shape, jnp.float32),
        in_specs=[smem, vmem, vmem],
        out_specs=pl.BlockSpec(memory_space=pl.ANY),
        scratch_shapes=[
            pltpu.VMEM(mixed_blocks.shape, jnp.float32),
            pltpu.SemaphoreType.DMA((clusters,)),
        ],
        compiler_params=pltpu.CompilerParams(vmem_limit_bytes=16 << 20),
    )(neighbours, grad, mixed_blocks)


def swap(x, axis):
    return lax.all_to_all(x, axis, split_axis=0, concat_axis=0, tiled=True)


def paired(x, bit, momenta):
    other = lax.ppermute(x, "mom", [(k, k ^ bit) for k in range(momenta)])
    return jnp.concatenate([x, other])


def shards(green, grad, coupling, occupation, offsets, neighbours, qtable):
    clusters, parts, orbits = green.shape[2:5]
    momenta = lax.axis_size("mom")
    plane = lax.axis_size("y") * lax.axis_size("x") * lax.axis_size("core")
    quads = lax.axis_size("zh") * momenta
    rows = clusters * parts * orbits // plane
    quad = plane // momenta
    shape = (momenta, quad, rows, orbits)
    pieces = swap(green.reshape(plane, rows, orbits), PLANE)
    rates = jnp.stack([1.0 + occupation, occupation])
    level = jnp.arange(1, quad + 1, dtype=jnp.int32)
    chosen = jnp.where(offsets == level[:, None], rates[:, None], 0.0)
    levels = jnp.sum(chosen[:, :, None] * coupling, axis=-1).reshape(2 * quad, momenta)
    table = paired(jnp.repeat(qtable, orbits // momenta, axis=1).astype(green.dtype), 2, momenta)
    here = swap(pieces, "mom")
    table = paired(table, 4, momenta)
    table = jnp.pad(table, ((0, 16 - momenta // 2), (0, 0)))
    here = jnp.concatenate([here.reshape(-1, orbits), table])
    before = lax.ppermute(here, LINE, [(z, z + 1) for z in range(quads - 1)])
    after = lax.ppermute(here, LINE, [(z + 1, z) for z in range(quads - 1)])
    total = mixed(levels, before, here, after, shape)
    total = swap(swap(total.reshape(plane, rows, orbits), "mom"), PLANE)
    out = dressed(neighbours, grad[0], total.reshape(clusters, parts, orbits, orbits))
    return out[None, None]


def solution(mesh):
    split = Mesh(mesh.devices.reshape(4, 4, 4, 2, 8), ("zh", "y", "x", "core", "mom"))
    energy = ("zh", "y", "x", "core")
    in_specs = (
        P("mom", energy, None, None, None, None),
        P("mom", None, None, None, None, None),
        P(),
        P(),
        P(),
        P(),
        P("mom", None),
    )
    out_specs = P("mom", energy, None, None, None, None)
    return jax.shard_map(shards, mesh=split, in_specs=in_specs, out_specs=out_specs, check_vma=False)
```

```python
import jax
import jax.numpy as jnp
from jax import lax
from jax.experimental import pallas as pl
from jax.experimental.pallas import tpu as pltpu
from jax.sharding import Mesh
from jax.sharding import PartitionSpec as P


PLANE = ("y", "x", "core")
LINE = ("zh", "mom")


def mix_kernel(levels, before, here, after, out, rows_of):
    momenta, quad, rows, lanes = out.shape
    shifts = levels.shape[0]
    half = rows // 2
    height = momenta * half
    body = momenta * quad * rows
    me = lax.axis_index("mom")
    sublane = lax.broadcasted_iota(jnp.int32, (half, lanes), 0)
    lane = lax.broadcasted_iota(jnp.int32, (half, lanes), 1)
    diagonal = sublane == lax.rem(lane, half)
    values = levels[...]
    strengths = [jnp.broadcast_to(values[:, q : q + 1], (shifts, lanes)) for q in range(momenta)]
    own = here[body:].astype(jnp.float32)
    lower = before[body:].astype(jnp.float32)
    upper = after[body:].astype(jnp.float32)
    odd = jnp.zeros(own.shape, jnp.int32) + (me & 1)
    partner = jnp.where(odd == 1, lower, upper)
    for i in range(momenta):
        table = partner if i >= momenta // 2 else own
        spot = i % (momenta // 2)
        index = jnp.broadcast_to(table[spot : spot + 1], (shifts, lanes))
        weight = jnp.zeros((shifts, lanes), jnp.float32)
        for q, strength in enumerate(strengths):
            weight = jnp.where(index == float(q), strength, weight)
        high = weight.astype(jnp.bfloat16).astype(jnp.float32)
        for n, part in enumerate((high, weight - high)):
            for d in range(shifts):
                spread = jnp.broadcast_to(part[d : d + 1], (half, lanes))
                block = jnp.where(diagonal, spread, 0.0).astype(jnp.bfloat16)
                start = n * height + i * half
                rows_of[start : start + half, d * lanes : (d + 1) * lanes] = block

    def near(j, e):
        if e < 0:
            source, e = before, e + quad
        elif e < quad:
            source = here
        else:
            source, e = after, e - quad
        start = (j * quad + e) * rows
        return jnp.concatenate([source[start : start + half], source[start + half : start + rows]], axis=1)

    spots = [((i & 1) << 1 | (i & 2) << 1 | (i & 4) >> 2) ^ me for i in range(momenta)]
    for e in range(quad):
        blocks = [near(j, e - level) for level in range(1, quad + 1) for j in range(momenta)]
        blocks += [near(j, e + level) for level in range(1, quad + 1) for j in range(momenta)]
        both = jnp.dot(rows_of[...], jnp.concatenate(blocks, axis=0), preferred_element_type=jnp.float32)
        total = (both[:height] + both[height:]).astype(out.dtype)
        for i in range(momenta):
            piece = total[i * half : (i + 1) * half]
            out[spots[i], e, :half] = piece[:, :lanes]
            out[spots[i], e, half:] = piece[:, lanes:]


def mixed(levels, before, here, after, shape):
    vmem = pl.BlockSpec(memory_space=pltpu.VMEM)
    momenta, _, rows, lanes = shape
    shifts = levels.shape[0]
    return pl.pallas_call(
        mix_kernel,
        out_shape=jax.ShapeDtypeStruct(shape, jnp.bfloat16),
        in_specs=[vmem] * 4,
        out_specs=vmem,
        scratch_shapes=[pltpu.VMEM((momenta * rows, shifts * lanes), jnp.bfloat16)],
        compiler_params=pltpu.CompilerParams(vmem_limit_bytes=16 << 20),
    )(levels, before, here, after)


def dress_kernel(neighbours, grad, near, out, result, done):
    clusters, listed = grad.shape[:2]
    orbits = out.shape[-1]
    copies = []
    for c in range(clusters):
        total = None
        for s in range(listed):
            spot = neighbours[s, c]
            re = near[spot, 0]
            im = near[spot, 1]
            d_re = grad[c, s, 0]
            d_im = grad[c, s, 1]
            left = jnp.concatenate([d_re, d_im], axis=1)
            middle = jnp.concatenate(
                [jnp.concatenate([re, im], axis=1), jnp.concatenate([-im, re], axis=1)], axis=0
            )
            right = jnp.concatenate([left, jnp.concatenate([-d_im, d_re], axis=1)], axis=0)
            prod = jnp.dot(left, middle, preferred_element_type=jnp.float32)
            high = prod.astype(jnp.bfloat16)
            low = (prod - high.astype(jnp.float32)).astype(jnp.bfloat16)
            part = lax.dot_general(
                jnp.concatenate([high, low], axis=0),
                right,
                (((1,), (1,)), ((), ())),
                preferred_element_type=jnp.float32,
            )
            part = part[:orbits] + part[orbits:]
            total = part if total is None else total + part
        result[c, 0] = total[:, :orbits]
        result[c, 1] = total[:, orbits:]
        copy = pltpu.make_async_copy(result.at[c], out.at[c], done.at[c])
        copy.start()
        copies.append(copy)
    for copy in copies:
        copy.wait()


def dressed(neighbours, grad, mixed_blocks):
    smem = pl.BlockSpec(memory_space=pltpu.SMEM)
    vmem = pl.BlockSpec(memory_space=pltpu.VMEM)
    clusters = grad.shape[0]
    return pl.pallas_call(
        dress_kernel,
        out_shape=jax.ShapeDtypeStruct(mixed_blocks.shape, jnp.float32),
        in_specs=[smem, vmem, vmem],
        out_specs=pl.BlockSpec(memory_space=pl.ANY),
        scratch_shapes=[
            pltpu.VMEM(mixed_blocks.shape, jnp.float32),
            pltpu.SemaphoreType.DMA((clusters,)),
        ],
        compiler_params=pltpu.CompilerParams(vmem_limit_bytes=16 << 20),
    )(neighbours, grad, mixed_blocks)


def swap(x, axis):
    return lax.all_to_all(x, axis, split_axis=0, concat_axis=0, tiled=True)


def paired(x, bit, momenta):
    other = lax.ppermute(x, "mom", [(k, k ^ bit) for k in range(momenta)])
    return jnp.concatenate([x, other])


def shards(green, grad, coupling, occupation, offsets, neighbours, qtable):
    clusters, parts, orbits = green.shape[2:5]
    momenta = lax.axis_size("mom")
    plane = lax.axis_size("y") * lax.axis_size("x") * lax.axis_size("core")
    quads = lax.axis_size("zh") * momenta
    rows = clusters * parts * orbits // plane
    quad = plane // momenta
    shape = (momenta, quad, rows, orbits)
    pieces = swap(green.reshape(plane, rows, orbits), PLANE)
    rates = jnp.stack([1.0 + occupation, occupation])
    level = jnp.arange(1, quad + 1, dtype=jnp.int32)
    active = jnp.where(offsets == level[:, None], rates[:, None], 0.0)
    levels = jnp.sum(active[:, :, None] * coupling, axis=-1).reshape(2 * quad, momenta)
    chosen = jnp.pad(neighbours.T, ((0, 0), (0, quad)))
    table = paired(jnp.repeat(qtable, orbits // momenta, axis=1).astype(green.dtype), 2, momenta)
    here = swap(pieces, "mom")
    table = paired(table, 4, momenta)
    table = jnp.pad(table, ((0, 16 - momenta // 2), (0, 0)))
    here = jnp.concatenate([here.reshape(-1, orbits), table])
    before = lax.ppermute(here, LINE, [(z, z + 1) for z in range(quads - 1)])
    after = lax.ppermute(here, LINE, [(z + 1, z) for z in range(quads - 1)])
    total = mixed(levels, before, here, after, shape)
    total = swap(swap(total.reshape(plane, rows, orbits), "mom"), PLANE)
    out = dressed(chosen, grad[0], total.reshape(clusters, parts, orbits, orbits))
    return out[None, None]


def solution(mesh):
    split = Mesh(mesh.devices.reshape(4, 4, 4, 2, 8), ("zh", "y", "x", "core", "mom"))
    energy = ("zh", "y", "x", "core")
    in_specs = (
        P("mom", energy, None, None, None, None),
        P("mom", None, None, None, None, None),
        P(),
        P(),
        P(),
        P(),
        P("mom", None),
    )
    out_specs = P("mom", energy, None, None, None, None)
    return jax.shard_map(shards, mesh=split, in_specs=in_specs, out_specs=out_specs, check_vma=False)
```

```python
import jax
import jax.numpy as jnp
from jax import lax
from jax.experimental import pallas as pl
from jax.experimental.pallas import tpu as pltpu
from jax.sharding import Mesh
from jax.sharding import PartitionSpec as P


PLANE = ("y", "x", "core")
LINE = ("zh", "mom")


def mix_kernel(levels, before, here, after, out, rows_of):
    momenta, quad, rows, lanes = out.shape
    shifts = levels.shape[0]
    half = rows // 2
    height = momenta * half
    body = momenta * quad * rows
    me = lax.axis_index("mom")
    sublane = lax.broadcasted_iota(jnp.int32, (half, lanes), 0)
    lane = lax.broadcasted_iota(jnp.int32, (half, lanes), 1)
    diagonal = sublane == lax.rem(lane, half)
    values = levels[...]
    strengths = [jnp.broadcast_to(values[:, q : q + 1], (shifts, lanes)) for q in range(momenta)]
    own = here[body:].astype(jnp.float32)
    lower = before[body:].astype(jnp.float32)
    upper = after[body:].astype(jnp.float32)
    odd = jnp.zeros(own.shape, jnp.int32) + (me & 1)
    partner = jnp.where(odd == 1, lower, upper)
    for i in range(momenta):
        table = partner if i >= momenta // 2 else own
        spot = i % (momenta // 2)
        index = jnp.broadcast_to(table[spot : spot + 1], (shifts, lanes))
        weight = jnp.zeros((shifts, lanes), jnp.float32)
        for q, strength in enumerate(strengths):
            weight = jnp.where(index == float(q), strength, weight)
        high = weight.astype(jnp.bfloat16).astype(jnp.float32)
        for n, part in enumerate((high, weight - high)):
            for d in range(shifts):
                spread = jnp.broadcast_to(part[d : d + 1], (half, lanes))
                block = jnp.where(diagonal, spread, 0.0).astype(jnp.bfloat16)
                start = n * height + i * half
                rows_of[start : start + half, d * lanes : (d + 1) * lanes] = block

    def near(j, e):
        if e < 0:
            source, e = before, e + quad
        elif e < quad:
            source = here
        else:
            source, e = after, e - quad
        start = (j * quad + e) * rows
        return jnp.concatenate([source[start : start + half], source[start + half : start + rows]], axis=1)

    spots = [((i & 1) << 1 | (i & 2) << 1 | (i & 4) >> 2) ^ me for i in range(momenta)]
    for e in range(quad):
        blocks = [near(j, e - level) for level in range(1, quad + 1) for j in range(momenta)]
        blocks += [near(j, e + level) for level in range(1, quad + 1) for j in range(momenta)]
        both = jnp.dot(rows_of[...], jnp.concatenate(blocks, axis=0), preferred_element_type=jnp.float32)
        total = (both[:height] + both[height:]).astype(out.dtype)
        for i in range(momenta):
            piece = total[i * half : (i + 1) * half]
            out[spots[i], e, :half] = piece[:, :lanes]
            out[spots[i], e, half:] = piece[:, lanes:]


def mixed(levels, before, here, after, shape):
    vmem = pl.BlockSpec(memory_space=pltpu.VMEM)
    momenta, _, rows, lanes = shape
    shifts = levels.shape[0]
    return pl.pallas_call(
        mix_kernel,
        out_shape=jax.ShapeDtypeStruct(shape, jnp.bfloat16),
        in_specs=[vmem] * 4,
        out_specs=vmem,
        scratch_shapes=[pltpu.VMEM((momenta * rows, shifts * lanes), jnp.bfloat16)],
        compiler_params=pltpu.CompilerParams(vmem_limit_bytes=16 << 20),
    )(levels, before, here, after)


def dress_kernel(neighbours, grad, near, out, result, done):
    clusters, listed = grad.shape[:2]
    orbits = out.shape[-1]
    copies = []
    for c in range(clusters):
        prods, rights = [], []
        for s in range(listed):
            spot = neighbours[s, c]
            re = near[spot, 0]
            im = near[spot, 1]
            d_re = grad[c, s, 0]
            d_im = grad[c, s, 1]
            left = jnp.concatenate([d_re, d_im], axis=1)
            middle = jnp.concatenate(
                [jnp.concatenate([re, im], axis=1), jnp.concatenate([-im, re], axis=1)], axis=0
            )
            rights.append(jnp.concatenate([left, jnp.concatenate([-d_im, d_re], axis=1)], axis=0))
            prods.append(jnp.dot(left, middle, preferred_element_type=jnp.float32))
        prod = jnp.concatenate(prods, axis=1)
        high = prod.astype(jnp.bfloat16)
        low = (prod - high.astype(jnp.float32)).astype(jnp.bfloat16)
        both = lax.dot_general(
            jnp.concatenate([high, low], axis=0),
            jnp.concatenate(rights, axis=1),
            (((1,), (1,)), ((), ())),
            preferred_element_type=jnp.float32,
        )
        total = both[:orbits] + both[orbits:]
        result[c, 0] = total[:, :orbits]
        result[c, 1] = total[:, orbits:]
        copy = pltpu.make_async_copy(result.at[c], out.at[c], done.at[c])
        copy.start()
        copies.append(copy)
    for copy in copies:
        copy.wait()


def dressed(neighbours, grad, mixed_blocks):
    smem = pl.BlockSpec(memory_space=pltpu.SMEM)
    vmem = pl.BlockSpec(memory_space=pltpu.VMEM)
    clusters = grad.shape[0]
    return pl.pallas_call(
        dress_kernel,
        out_shape=jax.ShapeDtypeStruct(mixed_blocks.shape, jnp.float32),
        in_specs=[smem, vmem, vmem],
        out_specs=pl.BlockSpec(memory_space=pl.ANY),
        scratch_shapes=[
            pltpu.VMEM(mixed_blocks.shape, jnp.float32),
            pltpu.SemaphoreType.DMA((clusters,)),
        ],
        compiler_params=pltpu.CompilerParams(vmem_limit_bytes=16 << 20),
    )(neighbours, grad, mixed_blocks)


def swap(x, axis):
    return lax.all_to_all(x, axis, split_axis=0, concat_axis=0, tiled=True)


def paired(x, bit, momenta):
    other = lax.ppermute(x, "mom", [(k, k ^ bit) for k in range(momenta)])
    return jnp.concatenate([x, other])


def shards(green, grad, coupling, occupation, offsets, neighbours, qtable):
    clusters, parts, orbits = green.shape[2:5]
    momenta = lax.axis_size("mom")
    plane = lax.axis_size("y") * lax.axis_size("x") * lax.axis_size("core")
    quads = lax.axis_size("zh") * momenta
    rows = clusters * parts * orbits // plane
    quad = plane // momenta
    shape = (momenta, quad, rows, orbits)
    pieces = swap(green.reshape(plane, rows, orbits), PLANE)
    rates = jnp.stack([1.0 + occupation, occupation])
    level = jnp.arange(1, quad + 1, dtype=jnp.int32)
    active = jnp.where(offsets == level[:, None], rates[:, None], 0.0)
    levels = jnp.sum(active[:, :, None] * coupling, axis=-1).reshape(2 * quad, momenta)
    chosen = jnp.pad(neighbours.T, ((0, 0), (0, quad)))
    table = paired(jnp.repeat(qtable, orbits // momenta, axis=1).astype(green.dtype), 2, momenta)
    here = swap(pieces, "mom")
    table = paired(table, 4, momenta)
    table = jnp.pad(table, ((0, 16 - momenta // 2), (0, 0)))
    here = jnp.concatenate([here.reshape(-1, orbits), table])
    before = lax.ppermute(here, LINE, [(z, z + 1) for z in range(quads - 1)])
    after = lax.ppermute(here, LINE, [(z + 1, z) for z in range(quads - 1)])
    total = mixed(levels, before, here, after, shape)
    total = swap(swap(total.reshape(plane, rows, orbits), "mom"), PLANE)
    out = dressed(chosen, grad[0], total.reshape(clusters, parts, orbits, orbits))
    return out[None, None]


def solution(mesh):
    split = Mesh(mesh.devices.reshape(4, 4, 4, 2, 8), ("zh", "y", "x", "core", "mom"))
    energy = ("zh", "y", "x", "core")
    in_specs = (
        P("mom", energy, None, None, None, None),
        P("mom", None, None, None, None, None),
        P(),
        P(),
        P(),
        P(),
        P("mom", None),
    )
    out_specs = P("mom", energy, None, None, None, None)
    return jax.shard_map(shards, mesh=split, in_specs=in_specs, out_specs=out_specs, check_vma=False)
```

```python
import jax
import jax.numpy as jnp
from jax import lax
from jax.experimental import pallas as pl
from jax.experimental.pallas import tpu as pltpu
from jax.sharding import Mesh
from jax.sharding import PartitionSpec as P


PLANE = ("y0", "xh", "y1", "xl", "core")
ENERGY = ("y1", "y0", "xh", "xl", "core")
MOM = ("m4", "m2", "m1")
FAR = ("m2", "m1", "m4")
LINE = ("zh", *MOM)


def mix_kernel(levels, before, here, after, out, rows_of):
    momenta, quad, rows, lanes = out.shape
    shifts = levels.shape[0]
    half = rows // 2
    height = momenta * half
    body = momenta * quad * rows
    me = lax.axis_index("m4") * 4 + lax.axis_index("m2") * 2 + lax.axis_index("m1")
    sublane = lax.broadcasted_iota(jnp.int32, (half, lanes), 0)
    lane = lax.broadcasted_iota(jnp.int32, (half, lanes), 1)
    diagonal = sublane == lax.rem(lane, half)
    values = levels[...]
    strengths = [jnp.broadcast_to(values[:, q : q + 1], (shifts, lanes)) for q in range(momenta)]
    own = here[body:].astype(jnp.float32)
    lower = before[body:].astype(jnp.float32)
    upper = after[body:].astype(jnp.float32)
    odd = jnp.zeros(own.shape, jnp.int32) + (me & 1)
    partner = jnp.where(odd == 1, lower, upper)
    for i in range(momenta):
        table = partner if i >= momenta // 2 else own
        spot = i % (momenta // 2)
        index = jnp.broadcast_to(table[spot : spot + 1], (shifts, lanes))
        weight = jnp.zeros((shifts, lanes), jnp.float32)
        for q, strength in enumerate(strengths):
            weight = jnp.where(index == float(q), strength, weight)
        high = weight.astype(jnp.bfloat16).astype(jnp.float32)
        for n, part in enumerate((high, weight - high)):
            for d in range(shifts):
                spread = jnp.broadcast_to(part[d : d + 1], (half, lanes))
                block = jnp.where(diagonal, spread, 0.0).astype(jnp.bfloat16)
                start = n * height + i * half
                rows_of[start : start + half, d * lanes : (d + 1) * lanes] = block

    def near(j, e):
        if e < 0:
            source, e = before, e + quad
        elif e < quad:
            source = here
        else:
            source, e = after, e - quad
        start = (j * quad + e) * rows
        return jnp.concatenate([source[start : start + half], source[start + half : start + rows]], axis=1)

    spots = []
    for i in range(momenta):
        k = ((i & 1) << 1 | (i & 2) << 1 | (i & 4) >> 2) ^ me
        spots.append((k & 3) * 2 + (k >> 2))
    for e in range(quad):
        blocks = [near(j, e - level) for level in range(1, quad + 1) for j in range(momenta)]
        blocks += [near(j, e + level) for level in range(1, quad + 1) for j in range(momenta)]
        both = jnp.dot(rows_of[...], jnp.concatenate(blocks, axis=0), preferred_element_type=jnp.float32)
        total = (both[:height] + both[height:]).astype(out.dtype)
        for i in range(momenta):
            piece = total[i * half : (i + 1) * half]
            out[spots[i], e, :half] = piece[:, :lanes]
            out[spots[i], e, half:] = piece[:, lanes:]


def mixed(levels, before, here, after, shape):
    vmem = pl.BlockSpec(memory_space=pltpu.VMEM)
    momenta, _, rows, lanes = shape
    shifts = levels.shape[0]
    return pl.pallas_call(
        mix_kernel,
        out_shape=jax.ShapeDtypeStruct(shape, jnp.bfloat16),
        in_specs=[vmem] * 4,
        out_specs=vmem,
        scratch_shapes=[pltpu.VMEM((momenta * rows, shifts * lanes), jnp.bfloat16)],
        compiler_params=pltpu.CompilerParams(vmem_limit_bytes=16 << 20),
    )(levels, before, here, after)


def dress_kernel(neighbours, grad, near, out, result, done):
    clusters, listed = grad.shape[:2]
    orbits = out.shape[-1]
    copies = []
    for c in range(clusters):
        prods, rights = [], []
        for s in range(listed):
            spot = neighbours[s, c]
            re = near[spot, 0]
            im = near[spot, 1]
            d_re = grad[c, s, 0]
            d_im = grad[c, s, 1]
            left = jnp.concatenate([d_re, d_im], axis=1)
            middle = jnp.concatenate(
                [jnp.concatenate([re, im], axis=1), jnp.concatenate([-im, re], axis=1)], axis=0
            )
            rights.append(jnp.concatenate([left, jnp.concatenate([-d_im, d_re], axis=1)], axis=0))
            prods.append(jnp.dot(left, middle, preferred_element_type=jnp.float32))
        prod = jnp.concatenate(prods, axis=1)
        high = prod.astype(jnp.bfloat16)
        low = (prod - high.astype(jnp.float32)).astype(jnp.bfloat16)
        both = lax.dot_general(
            jnp.concatenate([high, low], axis=0),
            jnp.concatenate(rights, axis=1),
            (((1,), (1,)), ((), ())),
            preferred_element_type=jnp.float32,
        )
        total = both[:orbits] + both[orbits:]
        result[c, 0] = total[:, :orbits]
        result[c, 1] = total[:, orbits:]
        copy = pltpu.make_async_copy(result.at[c], out.at[c], done.at[c])
        copy.start()
        copies.append(copy)
    for copy in copies:
        copy.wait()


def dressed(neighbours, grad, mixed_blocks):
    smem = pl.BlockSpec(memory_space=pltpu.SMEM)
    vmem = pl.BlockSpec(memory_space=pltpu.VMEM)
    clusters = grad.shape[0]
    return pl.pallas_call(
        dress_kernel,
        out_shape=jax.ShapeDtypeStruct(mixed_blocks.shape, jnp.float32),
        in_specs=[smem, vmem, vmem],
        out_specs=pl.BlockSpec(memory_space=pl.ANY),
        scratch_shapes=[
            pltpu.VMEM(mixed_blocks.shape, jnp.float32),
            pltpu.SemaphoreType.DMA((clusters,)),
        ],
        compiler_params=pltpu.CompilerParams(vmem_limit_bytes=16 << 20),
    )(neighbours, grad, mixed_blocks)


def swap(x, axis):
    return lax.all_to_all(x, axis, split_axis=0, concat_axis=0, tiled=True)


def paired(x, bit, momenta):
    other = lax.ppermute(x, MOM, [(k, k ^ bit) for k in range(momenta)])
    return jnp.concatenate([x, other])


def shards(green, grad, coupling, occupation, offsets, neighbours, qtable):
    clusters, parts, orbits = green.shape[2:5]
    momenta = coupling.shape[0]
    plane = 1
    for axis in PLANE:
        plane *= lax.axis_size(axis)
    quads = lax.axis_size("zh") * momenta
    rows = clusters * parts * orbits // plane
    quad = plane // momenta
    shape = (momenta, quad, rows, orbits)
    pieces = swap(green.reshape(plane, rows, orbits), PLANE)
    rates = jnp.stack([1.0 + occupation, occupation])
    level = jnp.arange(1, quad + 1, dtype=jnp.int32)
    active = jnp.where(offsets == level[:, None], rates[:, None], 0.0)
    levels = jnp.sum(active[:, :, None] * coupling, axis=-1).reshape(2 * quad, momenta)
    chosen = jnp.pad(neighbours.T, ((0, 0), (0, quad)))
    ordered = qtable.reshape(1, 2, 4).swapaxes(1, 2).reshape(1, momenta)
    table = paired(jnp.repeat(ordered, orbits // momenta, axis=1).astype(green.dtype), 2, momenta)
    here = swap(pieces, FAR)
    table = paired(table, 4, momenta)
    table = jnp.pad(table, ((0, 16 - momenta // 2), (0, 0)))
    here = jnp.concatenate([here.reshape(-1, orbits), table])
    before = lax.ppermute(here, LINE, [(z, z + 1) for z in range(quads - 1)])
    after = lax.ppermute(here, LINE, [(z + 1, z) for z in range(quads - 1)])
    total = mixed(levels, before, here, after, shape)
    total = swap(swap(total.reshape(plane, rows, orbits), FAR), PLANE)
    out = dressed(chosen, grad[0], total.reshape(clusters, parts, orbits, orbits))
    return out[None, None]


def solution(mesh):
    split = Mesh(mesh.devices.reshape(4, *[2] * 8), ("zh", *ENERGY, *MOM))
    energy = ("zh", *ENERGY)
    in_specs = (
        P(MOM, energy, None, None, None, None),
        P(MOM, None, None, None, None, None),
        P(),
        P(),
        P(),
        P(),
        P(MOM, None),
    )
    out_specs = P(MOM, energy, None, None, None, None)
    return jax.shard_map(shards, mesh=split, in_specs=in_specs, out_specs=out_specs, check_vma=False)
```

```python
import jax
import jax.numpy as jnp
from jax import lax
from jax.experimental import pallas as pl
from jax.experimental.pallas import tpu as pltpu
from jax.sharding import Mesh
from jax.sharding import PartitionSpec as P


PLANE = ("y", "x", "core")
LINE = ("zh", "mom")


def mix_kernel(levels, before, here, after, out, rows_of):
    momenta, quad, rows, lanes = out.shape
    shifts = levels.shape[0]
    half = rows // 2
    height = momenta * half
    body = momenta * quad * rows
    me = lax.axis_index("mom")
    sublane = lax.broadcasted_iota(jnp.int32, (half, lanes), 0)
    lane = lax.broadcasted_iota(jnp.int32, (half, lanes), 1)
    diagonal = sublane == lax.rem(lane, half)
    values = levels[...]
    strengths = [jnp.broadcast_to(values[:, q : q + 1], (shifts, lanes)) for q in range(momenta)]
    own = here[body:].astype(jnp.float32)
    lower = before[body:].astype(jnp.float32)
    upper = after[body:].astype(jnp.float32)
    odd = jnp.zeros(own.shape, jnp.int32) + (me & 1)
    partner = jnp.where(odd == 1, lower, upper)
    for i in range(momenta):
        table = partner if i >= momenta // 2 else own
        spot = i % (momenta // 2)
        index = jnp.broadcast_to(table[spot : spot + 1], (shifts, lanes))
        weight = jnp.zeros((shifts, lanes), jnp.float32)
        for q, strength in enumerate(strengths):
            weight = jnp.where(index == float(q), strength, weight)
        high = weight.astype(jnp.bfloat16).astype(jnp.float32)
        for n, part in enumerate((high, weight - high)):
            for d in range(shifts):
                spread = jnp.broadcast_to(part[d : d + 1], (half, lanes))
                block = jnp.where(diagonal, spread, 0.0).astype(jnp.bfloat16)
                start = n * height + i * half
                rows_of[start : start + half, d * lanes : (d + 1) * lanes] = block

    def near(j, e):
        if e < 0:
            source, e = before, e + quad
        elif e < quad:
            source = here
        else:
            source, e = after, e - quad
        start = (j * quad + e) * rows
        return jnp.concatenate([source[start : start + half], source[start + half : start + rows]], axis=1)

    spots = [((i & 1) << 1 | (i & 2) << 1 | (i & 4) >> 2) ^ me for i in range(momenta)]
    for e in range(quad):
        blocks = [near(j, e - level) for level in range(1, quad + 1) for j in range(momenta)]
        blocks += [near(j, e + level) for level in range(1, quad + 1) for j in range(momenta)]
        both = jnp.dot(rows_of[...], jnp.concatenate(blocks, axis=0), preferred_element_type=jnp.float32)
        total = (both[:height] + both[height:]).astype(out.dtype)
        for i in range(momenta):
            piece = total[i * half : (i + 1) * half]
            out[spots[i], e, :half] = piece[:, :lanes]
            out[spots[i], e, half:] = piece[:, lanes:]


def mixed(levels, before, here, after, shape):
    vmem = pl.BlockSpec(memory_space=pltpu.VMEM)
    momenta, _, rows, lanes = shape
    shifts = levels.shape[0]
    return pl.pallas_call(
        mix_kernel,
        out_shape=jax.ShapeDtypeStruct(shape, jnp.bfloat16),
        in_specs=[vmem] * 4,
        out_specs=vmem,
        scratch_shapes=[pltpu.VMEM((momenta * rows, shifts * lanes), jnp.bfloat16)],
        compiler_params=pltpu.CompilerParams(vmem_limit_bytes=16 << 20),
    )(levels, before, here, after)


def dress_kernel(chosen, grad, near, out, result, minus, neighbours, done, ready):
    clusters, listed = grad.shape[:2]
    orbits = out.shape[-1]
    copy = pltpu.make_async_copy(chosen, neighbours, ready)
    copy.start()
    for c in range(clusters):
        for s in range(listed):
            minus[c, s] = -grad[c, s, 1]
    copy.wait()
    copies = []
    for c in range(clusters):
        prods, rights = [], []
        for s in range(listed):
            spot = neighbours[s, c]
            re = near[spot, 0]
            im = near[spot, 1]
            d_re = grad[c, s, 0]
            d_im = grad[c, s, 1]
            left = jnp.concatenate([d_re, d_im], axis=1)
            middle = jnp.concatenate(
                [jnp.concatenate([re, im], axis=1), jnp.concatenate([-im, re], axis=1)], axis=0
            )
            rights.append(jnp.concatenate([left, jnp.concatenate([minus[c, s], d_re], axis=1)], axis=0))
            prods.append(jnp.dot(left, middle, preferred_element_type=jnp.float32))
        prod = jnp.concatenate(prods, axis=1)
        high = prod.astype(jnp.bfloat16)
        low = (prod - high.astype(jnp.float32)).astype(jnp.bfloat16)
        both = lax.dot_general(
            jnp.concatenate([high, low], axis=0),
            jnp.concatenate(rights, axis=1),
            (((1,), (1,)), ((), ())),
            preferred_element_type=jnp.float32,
        )
        total = both[:orbits] + both[orbits:]
        result[c, 0] = total[:, :orbits]
        result[c, 1] = total[:, orbits:]
        copy = pltpu.make_async_copy(result.at[c], out.at[c], done.at[c])
        copy.start()
        copies.append(copy)
    for copy in copies:
        copy.wait()


def dressed(neighbours, grad, mixed_blocks):
    free = pl.BlockSpec(memory_space=pl.ANY)
    vmem = pl.BlockSpec(memory_space=pltpu.VMEM)
    clusters = grad.shape[0]
    return pl.pallas_call(
        dress_kernel,
        out_shape=jax.ShapeDtypeStruct(mixed_blocks.shape, jnp.float32),
        in_specs=[free, vmem, vmem],
        out_specs=free,
        scratch_shapes=[
            pltpu.VMEM(mixed_blocks.shape, jnp.float32),
            pltpu.VMEM((clusters, grad.shape[1], *mixed_blocks.shape[2:]), grad.dtype),
            pltpu.SMEM(neighbours.shape, jnp.int32),
            pltpu.SemaphoreType.DMA((clusters,)),
            pltpu.SemaphoreType.DMA,
        ],
        compiler_params=pltpu.CompilerParams(vmem_limit_bytes=16 << 20),
    )(neighbours, grad, mixed_blocks)


def swap(x, axis):
    return lax.all_to_all(x, axis, split_axis=0, concat_axis=0, tiled=True)


def paired(x, bit, momenta):
    other = lax.ppermute(x, "mom", [(k, k ^ bit) for k in range(momenta)])
    return jnp.concatenate([x, other])


def shards(green, grad, coupling, occupation, offsets, neighbours, qtable):
    clusters, parts, orbits = green.shape[2:5]
    momenta = lax.axis_size("mom")
    plane = lax.axis_size("y") * lax.axis_size("x") * lax.axis_size("core")
    quads = lax.axis_size("zh") * momenta
    rows = clusters * parts * orbits // plane
    quad = plane // momenta
    shape = (momenta, quad, rows, orbits)
    pieces = swap(green.reshape(plane, rows, orbits), PLANE)
    rates = jnp.stack([1.0 + occupation, occupation])
    level = jnp.arange(1, quad + 1, dtype=jnp.int32)
    active = jnp.where(offsets == level[:, None], rates[:, None], 0.0)
    levels = jnp.sum(active[:, :, None] * coupling, axis=-1).reshape(2 * quad, momenta)
    chosen = jnp.pad(neighbours.T, ((0, 0), (0, quad)))
    table = paired(jnp.repeat(qtable, orbits // momenta, axis=1).astype(green.dtype), 2, momenta)
    here = swap(pieces, "mom")
    table = paired(table, 4, momenta)
    table = jnp.pad(table, ((0, 16 - momenta // 2), (0, 0)))
    here = jnp.concatenate([here.reshape(-1, orbits), table])
    before = lax.ppermute(here, LINE, [(z, z + 1) for z in range(quads - 1)])
    after = lax.ppermute(here, LINE, [(z + 1, z) for z in range(quads - 1)])
    total = mixed(levels, before, here, after, shape)
    total = swap(swap(total.reshape(plane, rows, orbits), "mom"), PLANE)
    out = dressed(chosen, grad[0], total.reshape(clusters, parts, orbits, orbits))
    return out[None, None]


def solution(mesh):
    split = Mesh(mesh.devices.reshape(4, 4, 4, 2, 8), ("zh", "y", "x", "core", "mom"))
    energy = ("zh", "y", "x", "core")
    in_specs = (
        P("mom", energy, None, None, None, None),
        P("mom", None, None, None, None, None),
        P(),
        P(),
        P(),
        P(),
        P("mom", None),
    )
    out_specs = P("mom", energy, None, None, None, None)
    return jax.shard_map(shards, mesh=split, in_specs=in_specs, out_specs=out_specs, check_vma=False)
```
